32 devices in a mesh: replica: 1, mp: 32 (over z, y, x, core), sub: 1.
Axes of the slice: x: 2, y: 2, z: 4, core: 2. Of those that a mesh axis runs over, the one named last changes fastest.
Arguments:
- hidden: bfloat16 [4, 128, 2, 4096], P(None, ('replica', 'mp'), 'sub'), may hold values from -300 to 300
- norm_gain: bfloat16 [2, 4096], P('sub'), may hold values from 0.5 to 1.5
- head_weight: bfloat16 [2, 4096, 32768], P('sub', None, 'mp'), may hold values from -0.09375 to 0.09375
- base_logits: bfloat16 [4, 128, 32768], P(None, ('replica', 'sub'), 'mp'), may hold values from -60 to 300
- tokens: int32 [4, 128], P(None, ('replica', 'sub')), may hold values from 0 to 32767
- cache_length: int32 [128], P(('replica', 'sub')), may hold values from 1 to 8192
Outputs:
- log_probs: float32 [4, 128, 32768], P(None, ('replica', 'sub'), 'mp')
- chosen: float32 [4, 128], P(None, ('replica', 'sub'))
- ranking: float32 [128], P(('replica', 'sub'))
The draws below stay inside these ranges and needn't reach their ends.
All inputs are finite; a program needn't handle non-finite values.
Results may differ from the reference program's by a relative error of at most 0.00047.
Values may be sent and summed in bfloat16 or wider, within the bound.
A program may use at most 64 MiB of HBM per device.

```python
import math
import jax
import jax.numpy as jnp
import numpy as np
from jax import lax

D = 4096
ROWS = 128
STEPS = 4
CTX = 8192
VOCAB = 32768


def rough_field(key, shape, clip_level):
    return jnp.clip(jax.random.normal(key, shape, jnp.float32), -clip_level, clip_level)


def draw_hidden(key, part):
    noise_key, row_key, feature_key = jax.random.split(key, 3)
    noise = rough_field(noise_key, (STEPS, ROWS, 2, D), 3.0)
    row_scale = jnp.exp(jax.random.uniform(row_key, (STEPS, ROWS, 2, 1), jnp.float32, 0.0, math.log(10.0)))
    feature_scale = jnp.exp(jax.random.uniform(feature_key, (1, 1, 2, D), jnp.float32, 0.0, math.log(10.0)))
    return (noise * row_scale * feature_scale).astype(jnp.bfloat16)


def draw_base_logits(key, part):
    keys = jax.random.split(key, 6)
    tilt = 1.1
    reach = 150.0
    positions = jnp.arange(VOCAB, dtype=jnp.int32)
    offset = tilt * (1.0 - positions.astype(jnp.float32) / VOCAB)
    noise = rough_field(keys[0], (STEPS, ROWS, VOCAB), 4.0)
    row_scale = jnp.exp(jax.random.uniform(keys[1], (STEPS, ROWS, 1), jnp.float32, 0.0, math.log(2.0)))
    column_scale = jnp.exp(jax.random.uniform(keys[2], (VOCAB,), jnp.float32, 0.0, math.log(5.0)))
    logits = offset + noise * row_scale * column_scale
    level = 100.0 + reach * jax.random.uniform(keys[3], (STEPS, ROWS, 1), jnp.float32)
    spacing = jax.random.uniform(keys[4], (STEPS, ROWS, 1), jnp.float32, 1.5, 3.0)
    target = jax.random.randint(keys[5], (STEPS, ROWS, 1), 0, VOCAB - 1)
    spiked = (jnp.arange(ROWS, dtype=jnp.int32) % 16 == 0)[None, :, None]
    columns = positions[None, None, :]
    logits = jnp.where(spiked & (columns == target), level, logits)
    logits = jnp.where(spiked & (columns == target + 1), level - spacing, logits)
    return logits.astype(jnp.bfloat16)


def set_ends(values, key, least, top_value):
    extent = values.shape
    index_at = [jax.random.randint(jax.random.fold_in(key, axis), (), 0, extent[axis]) for axis in range(len(extent))]
    values = values.at[tuple(index_at)].set(least)
    longest = extent.index(max(extent))
    index_at[longest] = (index_at[longest] + 1) % extent[longest]
    return values.at[tuple(index_at)].set(top_value)


def block_levels(stream_key, dims, pieces, smallest, largest):
    level = 1.0
    for position, blocks in pieces:
        steps = jax.random.uniform(jax.random.fold_in(jax.random.fold_in(stream_key, 6), position), (blocks,), jnp.float32, smallest / len(pieces), largest / len(pieces))
        level = level * jnp.repeat(jnp.exp(steps), dims[position] // blocks).reshape((-1,) + (1,) * (len(dims) - 1 - position))
    return level


def rank_table(number_of, skew):
    portions = [(1 << 20) // math.isqrt(grade ** skew) + 1 for grade in range(1, number_of + 1)]
    scale = 1 + sum(portions) // (1 << 30)
    return np.cumsum(np.array([max(1, weight // scale) for weight in portions]))


def skewed_ids(own_key, extent, count, skew):
    grid = rank_table(count, skew)
    ticket = jax.random.randint(jax.random.fold_in(own_key, 1), extent, 0, int(grid[count - 1]))
    grade = jnp.searchsorted(jnp.asarray(grid, jnp.int32), ticket, side="right")
    return jax.random.permutation(jax.random.fold_in(own_key, 2), count)[grade].astype(jnp.int32)


def normal_values(own_key, dims, scale, most, shards=(), kind=jnp.bfloat16):
    array = scale * jax.random.normal(own_key, dims, jnp.float32)
    if shards:
        array = array * block_levels(own_key, dims, shards, -0.22, 0.18)
    return jnp.clip(array, -most, most).astype(kind)


def setup_inputs(seed: int = 0, part: int = 0) -> dict:
    key_of = jax.random.split(jax.random.key(seed), 7)
    part_keys = jax.random.split(jax.random.fold_in(key_of[6], part), 7)
    return {
        "hidden": draw_hidden(jax.random.fold_in(jax.random.fold_in(key_of[6], part), 71), part),
        "norm_gain": jnp.clip(1.0 + 0.1 * jax.random.normal(key_of[1], (2, D), jnp.float32), 0.5, 1.5).astype(jnp.bfloat16),
        "head_weight": normal_values(key_of[2], (2, D, VOCAB), D ** -0.5, 0.09375, ((2, 32),)),
        "base_logits": draw_base_logits(jax.random.fold_in(jax.random.fold_in(key_of[6], part), 71), part),
        "tokens": set_ends(skewed_ids(part_keys[4], (STEPS, ROWS), VOCAB, 2), jax.random.fold_in(part_keys[4], 3), 0, VOCAB - 1).astype(jnp.int32),
        "cache_length": set_ends(jax.random.randint(part_keys[5], (ROWS,), 1, CTX + 1), jax.random.fold_in(part_keys[5], 1), 1, CTX).astype(jnp.int32),
    }


ALPHA = 2.0
EPSILON = 1e-05

def reference(hidden, norm_gain, head_weight, base_logits, tokens, cache_length):
    values = hidden.astype(jnp.float32)
    mean_square = lax.optimization_barrier(jnp.mean(values * values, axis=-1, keepdims=True))
    normed = (values * lax.rsqrt(mean_square + EPSILON) * norm_gain.astype(jnp.float32)[None, None]).astype(jnp.bfloat16)

    def one_step(inputs):
        normed_step, base_step, token_step = inputs
        expert = jnp.dot(normed_step[:, 0, :], head_weight[0], preferred_element_type=jnp.float32).astype(jnp.bfloat16)
        anti_expert = jnp.dot(normed_step[:, 1, :], head_weight[1], preferred_element_type=jnp.float32).astype(jnp.bfloat16)
        expert, anti_expert = lax.optimization_barrier((expert, anti_expert))
        combined = base_step.astype(jnp.float32) + ALPHA * (expert.astype(jnp.float32) - anti_expert.astype(jnp.float32))
        maximum = lax.optimization_barrier(jnp.max(combined, axis=-1))
        summed = lax.optimization_barrier(jnp.sum(jnp.exp(combined - maximum[:, None]), axis=-1))
        log_step = combined - maximum[:, None] - jnp.log(summed)[:, None]
        picked = jnp.take_along_axis(log_step, token_step[:, None].astype(jnp.int32), axis=1)[:, 0]
        return (log_step, picked)
    log_probs, chosen = lax.map(one_step, (normed, base_logits, tokens))
    penalty = ((5.0 + cache_length.astype(jnp.float32) + STEPS) / 6.0) ** 0.6
    ranking = lax.optimization_barrier(jnp.sum(chosen, axis=0)) / penalty
    return (log_probs, chosen, ranking)
```

```python
import functools

import jax
import jax.numpy as jnp
from jax import lax
from jax.experimental import pallas as pl
from jax.experimental.pallas import tpu as pltpu
from jax.sharding import PartitionSpec as P

ALPHA = 2.0
EPSILON = 1e-05


def score_block(normed, base_block, token_block, weights, slice_start):
    logits = jnp.einsum(
        "srmd,mdv->smrv",
        lax.all_gather(normed, "mp", axis=1, tiled=True),
        weights,
        preferred_element_type=jnp.float32,
    ).astype(jnp.bfloat16)
    step_count, model_count, row_count, vocab_width = logits.shape
    groups = lax.axis_size("sub")
    shares = logits.reshape(step_count, model_count, groups, row_count // groups, vocab_width)
    paired = lax.all_to_all(shares, "sub", split_axis=2, concat_axis=1, tiled=True)
    paired = paired.reshape(step_count, 2, row_count // groups, vocab_width)
    combined = base_block.astype(jnp.float32) + ALPHA * (
        paired[:, 0].astype(jnp.float32) - paired[:, 1].astype(jnp.float32)
    )
    columns = lax.broadcasted_iota(jnp.int32, (1, 1, vocab_width), 2) + slice_start
    picked_part = jnp.sum(jnp.where(columns == token_block[:, :, None], combined, 0.0), axis=2)
    maximum = lax.pmax(jnp.max(combined, axis=2), "mp")
    partial_value = jnp.sum(jnp.exp(combined - maximum[:, :, None]), axis=2)
    summed, picked = lax.psum((partial_value, picked_part), "mp")
    log_summed = jnp.log(summed)
    log_block = combined - maximum[:, :, None] - log_summed[:, :, None]
    chosen_block = picked - maximum - log_summed
    return (log_block, chosen_block)


def on_device(hidden, norm_gain, head_weight, base_logits, tokens, cache_length):
    step_count = hidden.shape[0]
    slice_start = lax.axis_index("mp") * head_weight.shape[2]
    values = hidden.astype(jnp.float32)
    mean_square = jnp.mean(values * values, axis=-1, keepdims=True)
    normed = (
        values * lax.rsqrt(mean_square + EPSILON) * norm_gain.astype(jnp.float32)[None, None]
    ).astype(jnp.bfloat16)
    log_parts = []
    chosen_parts = []
    for moment in range(step_count):
        log_block, chosen_block = score_block(
            normed[moment : moment + 1],
            base_logits[moment : moment + 1],
            tokens[moment : moment + 1],
            head_weight,
            slice_start,
        )
        log_parts.append(log_block)
        chosen_parts.append(chosen_block)
    log_probs = jnp.concatenate(log_parts, axis=0)
    chosen = jnp.concatenate(chosen_parts, axis=0)
    penalty = ((5.0 + cache_length.astype(jnp.float32) + step_count) / 6.0) ** 0.6
    ranking = jnp.sum(chosen, axis=0) / penalty
    return (log_probs, chosen, ranking)

CHUNKS = 8
AHEAD = 2
PLANE = 4
DEPTH = 4
CORES = 2


def remote(source, target, send_sem, recv_sem, device):
    return pltpu.make_async_remote_copy(
        src_ref=source,
        dst_ref=target,
        send_sem=send_sem,
        recv_sem=recv_sem,
        device_id={"mp": device},
        device_id_type=pl.DeviceIdType.MESH,
    )


def expert_kernel(
    normed,
    weight_hbm,
    base_hbm,
    tokens,
    cache_length,
    out,
    chosen_out,
    ranking_out,
    gathered,
    weight,
    acc,
    base,
    token_columns,
    stats,
    line_stats,
    plane_stats,
    weight_sem,
    base_sem,
    z_send,
    z_recv,
    x_send,
    x_recv,
    y_send,
    y_recv,
    dx_send,
    dx_recv,
    dy_send,
    dy_recv,
    s_send,
    s_recv,
    line_send,
    line_recv,
    plane_send,
    plane_recv,
):
    me = lax.axis_index("mp")
    z = me // 8
    q = (me // 2) % 4
    c = me % 2
    qx = q + 1 - 2 * (q % 2)
    qy = (q + 2) % 4
    qd = qx + 2 - 4 * (qx // 2)

    def device(zz, qq, cc):
        return zz * 8 + qq * 2 + cc

    x_device = device(z, qx, c)
    y_device = device(z, qy, c)
    sibling = device(z, q, 1 - c)
    blocks = CHUNKS // 2
    width = normed.shape[2]

    def weight_copy(chunk):
        return pltpu.make_async_copy(
            weight_hbm.at[chunk // blocks, pl.ds((chunk % blocks) * width, width), :],
            weight.at[chunk],
            weight_sem.at[chunk],
        )

    base_copy = pltpu.make_async_copy(base_hbm, base, base_sem)

    def z_copy(chunk, shift):
        peer = (z + shift) % DEPTH
        return remote(
            normed.at[chunk], gathered.at[chunk, q, c, z], z_send.at[chunk, peer], z_recv.at[chunk, z], device(peer, q, c)
        )

    def z_arrival(chunk, shift):
        peer = (z + shift) % DEPTH
        return remote(
            normed.at[chunk], gathered.at[chunk, q, c, peer], z_send.at[chunk, peer], z_recv.at[chunk, peer], device(peer, q, c)
        )

    def block_copy(chunk, block, send_sem, recv_sem, target):
        place = gathered.at[chunk, block, c]
        return remote(place, place, send_sem.at[chunk], recv_sem.at[chunk], target)

    def half_copy(chunk, block, start, send_sem, recv_sem, target):
        place = gathered.at[chunk, block, c, pl.ds(start, DEPTH // 2)]
        return remote(place, place, send_sem.at[chunk], recv_sem.at[chunk], target)

    def sibling_copy(chunk, block, core):
        place = gathered.at[chunk, block, core]
        return remote(place, place, s_send.at[chunk, block], s_recv.at[chunk, block], sibling)

    barrier = pltpu.get_barrier_semaphore()
    for shift in range(1, DEPTH):
        pl.semaphore_signal(barrier, inc=1, device_id={"mp": device((z + shift) % DEPTH, q, c)}, device_id_type=pl.DeviceIdType.MESH)
    for shift in range(1, PLANE * CORES):
        other = (me % 8 + shift) % 8
        pl.semaphore_signal(barrier, inc=1, device_id={"mp": z * 8 + other}, device_id_type=pl.DeviceIdType.MESH)

    @pl.loop(0, CHUNKS)
    def _(chunk):
        weight_copy(chunk).start()

    base_copy.start()
    pl.semaphore_wait(barrier, DEPTH - 1 + PLANE * CORES - 1)
    for chunk in range(AHEAD):
        for shift in range(1, DEPTH):
            z_copy(chunk, shift).start()

    @pl.loop(0, CHUNKS)
    def _(chunk):
        gathered[chunk, q, c, z] = normed[chunk]

    steps, rows, columns = out.shape
    diagonal = lax.broadcasted_iota(jnp.int32, (rows, rows), 0) == lax.broadcasted_iota(jnp.int32, (rows, rows), 1)

    def to_column(line):
        return jnp.sum(jnp.where(diagonal, jnp.broadcast_to(line, (rows, rows)), 0.0), axis=1, keepdims=True)

    def to_line(square):
        return jnp.sum(jnp.where(diagonal, square, 0.0), axis=0, keepdims=True)

    for step in range(steps):
        token_columns[step] = jnp.broadcast_to(to_column(tokens[step : step + 1, :].astype(jnp.float32)), (rows, rows))

    @pl.loop(0, CHUNKS + 3)
    def _(tick):
        @pl.when(tick < CHUNKS)
        def _():
            chunk = tick
            for shift in range(1, DEPTH):
                z_arrival(chunk, shift).wait_recv()
            block_copy(chunk, q, x_send, x_recv, x_device).start()
            block_copy(chunk, q, y_send, y_recv, y_device).start()
            sibling_copy(chunk, q, c).start()

        @pl.when(tick < CHUNKS - AHEAD)
        def _():
            for shift in range(1, DEPTH):
                z_copy(tick + AHEAD, shift).start()

        @pl.when(jnp.logical_and(tick >= 1, tick < CHUNKS + 1))
        def _():
            chunk = tick - 1
            block_copy(chunk, qx, x_send, x_recv, x_device).wait_recv()
            half_copy(chunk, qx, 0, dy_send, dy_recv, y_device).start()
            block_copy(chunk, qy, y_send, y_recv, y_device).wait_recv()
            half_copy(chunk, qy, DEPTH // 2, dx_send, dx_recv, x_device).start()
            sibling_copy(chunk, qx, c).start()
            sibling_copy(chunk, qy, c).start()

        @pl.when(jnp.logical_and(tick >= 2, tick < CHUNKS + 2))
        def _():
            chunk = tick - 2
            half_copy(chunk, qd, 0, dy_send, dy_recv, y_device).wait_recv()
            half_copy(chunk, qd, DEPTH // 2, dx_send, dx_recv, x_device).wait_recv()
            sibling_copy(chunk, qd, c).start()

        @pl.when(tick >= 3)
        def _():
            chunk = tick - 3
            for block in range(PLANE):
                sibling_copy(chunk, block, 1 - c).wait_recv()
            weight_copy(chunk).wait()
            model = chunk // blocks
            part = chunk % blocks
            count = gathered.shape[1] * gathered.shape[2] * gathered.shape[3] * gathered.shape[4]
            left = gathered[chunk].reshape(count, width)

            @pl.loop(0, columns // 256)
            def _(tile):
                at = pl.ds(pl.multiple_of(tile * 256, 256), 256)
                product = jnp.dot(left, weight[chunk, :, at], preferred_element_type=jnp.float32)

                @pl.when(part == 0)
                def _():
                    acc[model, :, at] = product

                @pl.when(part > 0)
                def _():
                    acc[model, :, at] += product

    base_copy.wait()
    slice_start = me * columns
    column = (lax.broadcasted_iota(jnp.int32, (16, columns), 1) + slice_start).astype(jnp.float32)
    low = lax.broadcasted_iota(jnp.int32, (8, columns), 0) < 4

    @pl.loop(0, rows // 16)
    def _(group):
        zz = group // 2
        pair = group % 2
        first = pl.multiple_of(group * 16, 16)
        parts = [[] for _ in range(steps)]
        for block in range(2):
            for tile in range(steps // 2):
                values = []
                for core in range(CORES):
                    place = pl.multiple_of((((pair * 2 + block) * CORES + core) * DEPTH + zz) * 16 + tile * 8, 8)
                    expert = acc[0, pl.ds(place, 8), :].astype(jnp.bfloat16).astype(jnp.float32)
                    anti = acc[1, pl.ds(place, 8), :].astype(jnp.bfloat16).astype(jnp.float32)
                    values.append(ALPHA * (expert - anti))
                parts[2 * tile].append(jnp.where(low, values[0], pltpu.roll(values[1], 4, 0)))
                parts[2 * tile + 1].append(jnp.where(low, pltpu.roll(values[0], 4, 0), values[1]))
        for step in range(steps):
            combined = base[step, pl.ds(first, 16), :].astype(jnp.float32) + jnp.concatenate(parts[step], axis=0)
            out[step, pl.ds(first, 16), :] = combined
            peak = jnp.max(combined, axis=1, keepdims=True)
            total = jnp.sum(jnp.exp(combined - peak), axis=1, keepdims=True)
            token = token_columns[step, pl.ds(first, 16), :][:, 0:1]
            picked = jnp.sum(jnp.where(column == token, combined, 0.0), axis=1, keepdims=True)
            stats[0, step, pl.ds(first, 16), :] = jnp.broadcast_to(peak, (16, rows))
            stats[1, step, pl.ds(first, 16), :] = jnp.broadcast_to(total, (16, rows))
            stats[2, step, pl.ds(first, 16), :] = jnp.broadcast_to(picked, (16, rows))

    for kind in range(3):
        for step in range(steps):
            line_stats[z, pl.ds(kind * steps + step, 1), :] = to_line(stats[kind, step])

    def line_copy(shift):
        peer = (z + shift) % DEPTH
        return remote(line_stats.at[z], line_stats.at[z], line_send.at[peer], line_recv.at[z], device(peer, q, c))

    def line_arrival(shift):
        peer = (z + shift) % DEPTH
        return remote(line_stats.at[peer], line_stats.at[peer], line_send.at[peer], line_recv.at[peer], device(peer, q, c))

    spot = me % 8

    def plane_copy(shift):
        peer = (spot + shift) % 8
        return remote(plane_stats.at[spot], plane_stats.at[spot], plane_send.at[peer], plane_recv.at[spot], z * 8 + peer)

    def plane_arrival(shift):
        peer = (spot + shift) % 8
        return remote(plane_stats.at[peer], plane_stats.at[peer], plane_send.at[peer], plane_recv.at[peer], z * 8 + peer)

    def merge(ref, count):
        peaks = [ref[index, 0:steps, :] for index in range(count)]
        peak = functools.reduce(jnp.maximum, peaks)
        total = sum(ref[index, steps : 2 * steps, :] * jnp.exp(peaks[index] - peak) for index in range(count))
        picked = sum(ref[index, 2 * steps : 3 * steps, :] for index in range(count))
        return peak, total, picked

    for shift in range(1, DEPTH):
        line_copy(shift).start()
    for shift in range(1, DEPTH):
        line_arrival(shift).wait_recv()
    for index, value in enumerate(merge(line_stats, DEPTH)):
        plane_stats[spot, pl.ds(index * steps, steps), :] = value
    for shift in range(1, 8):
        plane_copy(shift).start()
    for shift in range(1, 8):
        plane_arrival(shift).wait_recv()
    peak, total, picked = merge(plane_stats, 8)
    log_total = jnp.log(total)
    chosen = (picked - peak) - log_total
    chosen_out[...] = chosen
    penalty = jnp.exp(0.6 * jnp.log((5.0 + cache_length[...].astype(jnp.float32) + steps) / 6.0))
    ranking_out[...] = jnp.sum(chosen, axis=0, keepdims=True) / penalty
    for step in range(steps):
        peak_column = to_column(peak[step : step + 1, :])
        log_column = to_column(log_total[step : step + 1, :])
        out[step] = (out[step] - peak_column) - log_column

    for shift in range(1, DEPTH):
        line_copy(shift).wait_send()
    for shift in range(1, 8):
        plane_copy(shift).wait_send()

    @pl.loop(0, CHUNKS)
    def _(chunk):
        for shift in range(1, DEPTH):
            z_copy(chunk, shift).wait_send()
        block_copy(chunk, q, x_send, x_recv, x_device).wait_send()
        block_copy(chunk, q, y_send, y_recv, y_device).wait_send()
        half_copy(chunk, qx, 0, dy_send, dy_recv, y_device).wait_send()
        half_copy(chunk, qy, DEPTH // 2, dx_send, dx_recv, x_device).wait_send()
        for block in range(PLANE):
            sibling_copy(chunk, block, c).wait_send()


def on_box(hidden, norm_gain, head_weight, base_logits, tokens, cache_length):
    steps, own, models, features = hidden.shape
    rows, columns = base_logits.shape[1:]
    values = hidden.astype(jnp.float32)
    mean_square = jnp.mean(values * values, axis=-1, keepdims=True)
    normed = (
        values * lax.rsqrt(mean_square + EPSILON) * norm_gain.astype(jnp.float32)[None, None]
    ).astype(jnp.bfloat16)
    width = features * models // CHUNKS
    normed = normed.reshape(steps * own, models * features // width, width).transpose(1, 0, 2)
    any_space = pl.BlockSpec(memory_space=pl.ANY)
    local = pl.BlockSpec(memory_space=pltpu.VMEM)
    chunk_sems = pltpu.SemaphoreType.DMA((CHUNKS,))
    log_probs, chosen, ranking = pl.pallas_call(
        expert_kernel,
        out_shape=(
            jax.ShapeDtypeStruct((steps, rows, columns), jnp.float32),
            jax.ShapeDtypeStruct((steps, rows), jnp.float32),
            jax.ShapeDtypeStruct((1, rows), jnp.float32),
        ),
        in_specs=[local, any_space, any_space, local, local],
        out_specs=(local, local, local),
        scratch_shapes=[
            pltpu.VMEM((CHUNKS, PLANE, CORES, DEPTH, steps * own, width), jnp.bfloat16),
            pltpu.VMEM((CHUNKS, width, columns), jnp.bfloat16),
            pltpu.VMEM((models, steps * rows, columns), jnp.float32),
            pltpu.VMEM((steps, rows, columns), jnp.bfloat16),
            pltpu.VMEM((steps, rows, rows), jnp.float32),
            pltpu.VMEM((3, steps, rows, rows), jnp.float32),
            pltpu.VMEM((DEPTH, 3 * steps, rows), jnp.float32),
            pltpu.VMEM((PLANE * CORES, 3 * steps, rows), jnp.float32),
            chunk_sems,
            pltpu.SemaphoreType.DMA,
            pltpu.SemaphoreType.DMA((CHUNKS, DEPTH)),
            pltpu.SemaphoreType.DMA((CHUNKS, DEPTH)),
            chunk_sems,
            chunk_sems,
            chunk_sems,
            chunk_sems,
            chunk_sems,
            chunk_sems,
            chunk_sems,
            chunk_sems,
            pltpu.SemaphoreType.DMA((CHUNKS, PLANE)),
            pltpu.SemaphoreType.DMA((CHUNKS, PLANE)),
            pltpu.SemaphoreType.DMA((DEPTH,)),
            pltpu.SemaphoreType.DMA((DEPTH,)),
            pltpu.SemaphoreType.DMA((PLANE * CORES,)),
            pltpu.SemaphoreType.DMA((PLANE * CORES,)),
        ],
        compiler_params=pltpu.CompilerParams(
            collective_id=0, has_side_effects=True, vmem_limit_bytes=52 << 20
        ),
        name="experts",
    )(normed, head_weight, base_logits, tokens, cache_length.reshape(1, rows))
    return (log_probs, chosen, ranking.reshape(rows))


def fits_box(mesh):
    return mesh.shape["replica"] == 1 and mesh.shape["sub"] == 1 and mesh.shape["mp"] == PLANE * DEPTH * CORES


def solution(mesh):
    return jax.shard_map(
        on_box if fits_box(mesh) else on_device,
        mesh=mesh,
        in_specs=(
            P(None, ("replica", "mp"), "sub", None),
            P("sub", None),
            P("sub", None, "mp"),
            P(None, ("replica", "sub"), "mp"),
            P(None, ("replica", "sub")),
            P(("replica", "sub")),
        ),
        out_specs=(
            P(None, ("replica", "sub"), "mp"),
            P(None, ("replica", "sub")),
            P(("replica", "sub")),
        ),
        check_vma=False,
    )
```

```python
import functools

import jax
import jax.numpy as jnp
from jax import lax
from jax.experimental import pallas as pl
from jax.experimental.pallas import tpu as pltpu
from jax.sharding import PartitionSpec as P

ALPHA = 2.0
EPSILON = 1e-05


def score_block(normed, base_block, token_block, weights, slice_start):
    logits = jnp.einsum(
        "srmd,mdv->smrv",
        lax.all_gather(normed, "mp", axis=1, tiled=True),
        weights,
        preferred_element_type=jnp.float32,
    ).astype(jnp.bfloat16)
    step_count, model_count, row_count, vocab_width = logits.shape
    groups = lax.axis_size("sub")
    shares = logits.reshape(step_count, model_count, groups, row_count // groups, vocab_width)
    paired = lax.all_to_all(shares, "sub", split_axis=2, concat_axis=1, tiled=True)
    paired = paired.reshape(step_count, 2, row_count // groups, vocab_width)
    combined = base_block.astype(jnp.float32) + ALPHA * (
        paired[:, 0].astype(jnp.float32) - paired[:, 1].astype(jnp.float32)
    )
    columns = lax.broadcasted_iota(jnp.int32, (1, 1, vocab_width), 2) + slice_start
    picked_part = jnp.sum(jnp.where(columns == token_block[:, :, None], combined, 0.0), axis=2)
    maximum = lax.pmax(jnp.max(combined, axis=2), "mp")
    partial_value = jnp.sum(jnp.exp(combined - maximum[:, :, None]), axis=2)
    summed, picked = lax.psum((partial_value, picked_part), "mp")
    log_summed = jnp.log(summed)
    log_block = combined - maximum[:, :, None] - log_summed[:, :, None]
    chosen_block = picked - maximum - log_summed
    return (log_block, chosen_block)


def on_device(hidden, norm_gain, head_weight, base_logits, tokens, cache_length):
    step_count = hidden.shape[0]
    slice_start = lax.axis_index("mp") * head_weight.shape[2]
    values = hidden.astype(jnp.float32)
    mean_square = jnp.mean(values * values, axis=-1, keepdims=True)
    normed = (
        values * lax.rsqrt(mean_square + EPSILON) * norm_gain.astype(jnp.float32)[None, None]
    ).astype(jnp.bfloat16)
    log_parts = []
    chosen_parts = []
    for moment in range(step_count):
        log_block, chosen_block = score_block(
            normed[moment : moment + 1],
            base_logits[moment : moment + 1],
            tokens[moment : moment + 1],
            head_weight,
            slice_start,
        )
        log_parts.append(log_block)
        chosen_parts.append(chosen_block)
    log_probs = jnp.concatenate(log_parts, axis=0)
    chosen = jnp.concatenate(chosen_parts, axis=0)
    penalty = ((5.0 + cache_length.astype(jnp.float32) + step_count) / 6.0) ** 0.6
    ranking = jnp.sum(chosen, axis=0) / penalty
    return (log_probs, chosen, ranking)

CHUNKS = 8
AHEAD = 2
PLANE = 4
DEPTH = 4
CORES = 2


def remote(source, target, send_sem, recv_sem, device):
    return pltpu.make_async_remote_copy(
        src_ref=source,
        dst_ref=target,
        send_sem=send_sem,
        recv_sem=recv_sem,
        device_id={"mp": device},
        device_id_type=pl.DeviceIdType.MESH,
    )


def diagonal_of(rows):
    return lax.broadcasted_iota(jnp.int32, (rows, rows), 0) == lax.broadcasted_iota(jnp.int32, (rows, rows), 1)


def to_column(line, diagonal):
    square = jnp.broadcast_to(line, diagonal.shape)
    return jnp.sum(jnp.where(diagonal, square, 0.0), axis=1, keepdims=True)


def finish_kernel(combined, merged, cache_length, out_hbm, chosen_out, ranking_out, out, out_sem):
    steps, rows = chosen_out.shape
    diagonal = diagonal_of(rows)
    log_total = jnp.log(merged[steps : 2 * steps, :])
    copies = []
    for step in range(steps):
        peak_column = to_column(merged[step : step + 1, :], diagonal)
        log_column = to_column(log_total[step : step + 1, :], diagonal)
        out[step] = (combined[step] - peak_column) - log_column
        copies.append(pltpu.make_async_copy(out.at[step], out_hbm.at[step], out_sem.at[step]))
        copies[-1].start()
    chosen = (merged[2 * steps : 3 * steps, :] - merged[0:steps, :]) - log_total
    chosen_out[...] = chosen
    penalty = jnp.exp(0.6 * jnp.log((5.0 + cache_length[...].astype(jnp.float32) + steps) / 6.0))
    ranking_out[...] = jnp.sum(chosen, axis=0, keepdims=True) / penalty
    for copy in copies:
        copy.wait()


def expert_kernel(
    hidden_hbm,
    gain_hbm,
    weight_hbm,
    base_hbm,
    tokens_hbm,
    out,
    merged_out,
    hidden,
    gain,
    tokens,
    values,
    gathered,
    weight,
    acc,
    base,
    token_columns,
    stats,
    line_stats,
    plane_stats,
    hidden_sem,
    gain_sem,
    tokens_sem,
    weight_sem,
    base_sem,
    z_send,
    z_recv,
    x_send,
    x_recv,
    y_send,
    y_recv,
    dx_send,
    dx_recv,
    dy_send,
    dy_recv,
    s_send,
    s_recv,
    line_send,
    line_recv,
    plane_send,
    plane_recv,
):
    me = lax.axis_index("mp")
    z = me // 8
    q = (me // 2) % 4
    c = me % 2
    qx = q + 1 - 2 * (q % 2)
    qy = (q + 2) % 4
    qd = qx + 2 - 4 * (qx // 2)

    def device(zz, qq, cc):
        return zz * 8 + qq * 2 + cc

    x_device = device(z, qx, c)
    y_device = device(z, qy, c)
    sibling = device(z, q, 1 - c)
    blocks = CHUNKS // 2
    width = gathered.shape[5]
    hidden_copy = pltpu.make_async_copy(hidden_hbm, hidden, hidden_sem)
    gain_copy = pltpu.make_async_copy(gain_hbm, gain, gain_sem)
    tokens_copy = pltpu.make_async_copy(tokens_hbm, tokens, tokens_sem)
    hidden_copy.start()
    gain_copy.start()

    def weight_copy(chunk):
        return pltpu.make_async_copy(
            weight_hbm.at[chunk // blocks, pl.ds((chunk % blocks) * width, width), :],
            weight.at[chunk],
            weight_sem.at[chunk],
        )

    base_copy = pltpu.make_async_copy(base_hbm, base, base_sem)

    def z_copy(chunk, shift):
        peer = (z + shift) % DEPTH
        return remote(
            gathered.at[chunk, q, c, z], gathered.at[chunk, q, c, z], z_send.at[chunk, peer], z_recv.at[chunk, z], device(peer, q, c)
        )

    def z_arrival(chunk, shift):
        peer = (z + shift) % DEPTH
        return remote(
            gathered.at[chunk, q, c, peer], gathered.at[chunk, q, c, peer], z_send.at[chunk, peer], z_recv.at[chunk, peer], device(peer, q, c)
        )

    def block_copy(chunk, block, send_sem, recv_sem, target):
        place = gathered.at[chunk, block, c]
        return remote(place, place, send_sem.at[chunk], recv_sem.at[chunk], target)

    def half_copy(chunk, block, start, send_sem, recv_sem, target):
        place = gathered.at[chunk, block, c, pl.ds(start, DEPTH // 2)]
        return remote(place, place, send_sem.at[chunk], recv_sem.at[chunk], target)

    def sibling_copy(chunk, block, core):
        place = gathered.at[chunk, block, core]
        return remote(place, place, s_send.at[chunk, block], s_recv.at[chunk, block], sibling)

    barrier = pltpu.get_barrier_semaphore()
    for shift in range(1, DEPTH):
        pl.semaphore_signal(barrier, inc=1, device_id={"mp": device((z + shift) % DEPTH, q, c)}, device_id_type=pl.DeviceIdType.MESH)
    for shift in range(1, PLANE * CORES):
        other = (me % 8 + shift) % 8
        pl.semaphore_signal(barrier, inc=1, device_id={"mp": z * 8 + other}, device_id_type=pl.DeviceIdType.MESH)

    @pl.loop(0, CHUNKS)
    def _(chunk):
        weight_copy(chunk).start()

    base_copy.start()
    tokens_copy.start()
    hidden_copy.wait()
    gain_copy.wait()
    steps, own, models, features = hidden.shape
    for row in range(steps * own):
        pair = hidden[row // own, row % own].astype(jnp.float32)
        for model in range(models):
            values[model, row : row + 1, :] = pair[model : model + 1, :]
    for model in range(models):
        value = values[model]
        mean_square = jnp.mean(value * value, axis=-1, keepdims=True)
        scaled = value * lax.rsqrt(mean_square + EPSILON) * gain[model : model + 1, :].astype(jnp.float32)
        for part in range(blocks):
            gathered[model * blocks + part, q, c, z] = scaled[:, part * width : (part + 1) * width].astype(jnp.bfloat16)
    pl.semaphore_wait(barrier, DEPTH - 1 + PLANE * CORES - 1)
    for chunk in range(AHEAD):
        for shift in range(1, DEPTH):
            z_copy(chunk, shift).start()
    tokens_copy.wait()
    rows, columns = out.shape[1:]
    diagonal = diagonal_of(rows)

    def to_line(square):
        return jnp.sum(jnp.where(diagonal, square, 0.0), axis=0, keepdims=True)

    for step in range(steps):
        token_columns[step] = jnp.broadcast_to(to_column(tokens[step : step + 1, :].astype(jnp.float32), diagonal), (rows, rows))

    @pl.loop(0, CHUNKS + 3)
    def _(tick):
        @pl.when(tick < CHUNKS)
        def _():
            chunk = tick
            for shift in range(1, DEPTH):
                z_arrival(chunk, shift).wait_recv()
            block_copy(chunk, q, x_send, x_recv, x_device).start()
            block_copy(chunk, q, y_send, y_recv, y_device).start()
            sibling_copy(chunk, q, c).start()

        @pl.when(tick < CHUNKS - AHEAD)
        def _():
            for shift in range(1, DEPTH):
                z_copy(tick + AHEAD, shift).start()

        @pl.when(jnp.logical_and(tick >= 1, tick < CHUNKS + 1))
        def _():
            chunk = tick - 1
            block_copy(chunk, qx, x_send, x_recv, x_device).wait_recv()
            half_copy(chunk, qx, 0, dy_send, dy_recv, y_device).start()
            block_copy(chunk, qy, y_send, y_recv, y_device).wait_recv()
            half_copy(chunk, qy, DEPTH // 2, dx_send, dx_recv, x_device).start()
            sibling_copy(chunk, qx, c).start()
            sibling_copy(chunk, qy, c).start()

        @pl.when(jnp.logical_and(tick >= 2, tick < CHUNKS + 2))
        def _():
            chunk = tick - 2
            half_copy(chunk, qd, 0, dy_send, dy_recv, y_device).wait_recv()
            half_copy(chunk, qd, DEPTH // 2, dx_send, dx_recv, x_device).wait_recv()
            sibling_copy(chunk, qd, c).start()

        @pl.when(tick >= 3)
        def _():
            chunk = tick - 3
            for block in range(PLANE):
                sibling_copy(chunk, block, 1 - c).wait_recv()
            weight_copy(chunk).wait()
            model = chunk // blocks
            part = chunk % blocks
            count = gathered.shape[1] * gathered.shape[2] * gathered.shape[3] * gathered.shape[4]
            left = gathered[chunk].reshape(count, width)

            @pl.loop(0, columns // 256)
            def _(tile):
                at = pl.ds(pl.multiple_of(tile * 256, 256), 256)
                product = jnp.dot(left, weight[chunk, :, at], preferred_element_type=jnp.float32)

                @pl.when(part == 0)
                def _():
                    acc[model, :, at] = product

                @pl.when(part > 0)
                def _():
                    acc[model, :, at] += product

    base_copy.wait()
    slice_start = me * columns
    column = (lax.broadcasted_iota(jnp.int32, (16, columns), 1) + slice_start).astype(jnp.float32)
    low = lax.broadcasted_iota(jnp.int32, (8, columns), 0) < 4

    @pl.loop(0, rows // 16)
    def _(group):
        zz = group // 2
        pair = group % 2
        first = pl.multiple_of(group * 16, 16)
        parts = [[] for _ in range(steps)]
        for block in range(2):
            for tile in range(steps // 2):
                values = []
                for core in range(CORES):
                    place = pl.multiple_of((((pair * 2 + block) * CORES + core) * DEPTH + zz) * 16 + tile * 8, 8)
                    expert = acc[0, pl.ds(place, 8), :].astype(jnp.bfloat16).astype(jnp.float32)
                    anti = acc[1, pl.ds(place, 8), :].astype(jnp.bfloat16).astype(jnp.float32)
                    values.append(ALPHA * (expert - anti))
                parts[2 * tile].append(jnp.where(low, values[0], pltpu.roll(values[1], 4, 0)))
                parts[2 * tile + 1].append(jnp.where(low, pltpu.roll(values[0], 4, 0), values[1]))
        for step in range(steps):
            combined = base[step, pl.ds(first, 16), :].astype(jnp.float32) + jnp.concatenate(parts[step], axis=0)
            out[step, pl.ds(first, 16), :] = combined
            peak = jnp.max(combined, axis=1, keepdims=True)
            total = jnp.sum(jnp.exp(combined - peak), axis=1, keepdims=True)
            token = token_columns[step, pl.ds(first, 16), :][:, 0:1]
            picked = jnp.sum(jnp.where(column == token, combined, 0.0), axis=1, keepdims=True)
            stats[0, step, pl.ds(first, 16), :] = jnp.broadcast_to(peak, (16, rows))
            stats[1, step, pl.ds(first, 16), :] = jnp.broadcast_to(total, (16, rows))
            stats[2, step, pl.ds(first, 16), :] = jnp.broadcast_to(picked, (16, rows))

    for kind in range(3):
        for step in range(steps):
            line_stats[z, pl.ds(kind * steps + step, 1), :] = to_line(stats[kind, step])

    def line_copy(shift):
        peer = (z + shift) % DEPTH
        return remote(line_stats.at[z], line_stats.at[z], line_send.at[peer], line_recv.at[z], device(peer, q, c))

    def line_arrival(shift):
        peer = (z + shift) % DEPTH
        return remote(line_stats.at[peer], line_stats.at[peer], line_send.at[peer], line_recv.at[peer], device(peer, q, c))

    spot = me % 8

    def plane_copy(shift):
        peer = (spot + shift) % 8
        return remote(plane_stats.at[spot], plane_stats.at[spot], plane_send.at[peer], plane_recv.at[spot], z * 8 + peer)

    def plane_arrival(shift):
        peer = (spot + shift) % 8
        return remote(plane_stats.at[peer], plane_stats.at[peer], plane_send.at[peer], plane_recv.at[peer], z * 8 + peer)

    def merge(ref, count):
        peaks = [ref[index, 0:steps, :] for index in range(count)]
        peak = functools.reduce(jnp.maximum, peaks)
        total = sum(ref[index, steps : 2 * steps, :] * jnp.exp(peaks[index] - peak) for index in range(count))
        picked = sum(ref[index, 2 * steps : 3 * steps, :] for index in range(count))
        return peak, total, picked

    for shift in range(1, DEPTH):
        line_copy(shift).start()
    for shift in range(1, DEPTH):
        line_arrival(shift).wait_recv()
    for index, value in enumerate(merge(line_stats, DEPTH)):
        plane_stats[spot, pl.ds(index * steps, steps), :] = value
    for shift in range(1, 8):
        plane_copy(shift).start()
    for shift in range(1, 8):
        plane_arrival(shift).wait_recv()
    for index, value in enumerate(merge(plane_stats, 8)):
        merged_out[index * steps : (index + 1) * steps, :] = value

    for shift in range(1, DEPTH):
        line_copy(shift).wait_send()
    for shift in range(1, 8):
        plane_copy(shift).wait_send()

    @pl.loop(0, CHUNKS)
    def _(chunk):
        for shift in range(1, DEPTH):
            z_copy(chunk, shift).wait_send()
        block_copy(chunk, q, x_send, x_recv, x_device).wait_send()
        block_copy(chunk, q, y_send, y_recv, y_device).wait_send()
        half_copy(chunk, qx, 0, dy_send, dy_recv, y_device).wait_send()
        half_copy(chunk, qy, DEPTH // 2, dx_send, dx_recv, x_device).wait_send()
        for block in range(PLANE):
            sibling_copy(chunk, block, c).wait_send()


def on_box(hidden, norm_gain, head_weight, base_logits, tokens, cache_length):
    steps, own, models, features = hidden.shape
    rows, columns = base_logits.shape[1:]
    width = features * models // CHUNKS
    far = pl.BlockSpec(memory_space=pltpu.HBM)
    local = pl.BlockSpec(memory_space=pltpu.VMEM)
    chunk_sems = pltpu.SemaphoreType.DMA((CHUNKS,))
    line_sems = pltpu.SemaphoreType.DMA((DEPTH,))
    plane_sems = pltpu.SemaphoreType.DMA((PLANE * CORES,))
    each_sems = pltpu.SemaphoreType.DMA((CHUNKS, DEPTH))
    one_sem = pltpu.SemaphoreType.DMA
    combined, merged = pl.pallas_call(
        expert_kernel,
        out_shape=(
            jax.ShapeDtypeStruct((steps, rows, columns), jnp.float32),
            jax.ShapeDtypeStruct((3 * steps, rows), jnp.float32),
        ),
        in_specs=[far] * 5,
        out_specs=(local, local),
        scratch_shapes=[
            pltpu.VMEM(hidden.shape, jnp.bfloat16),
            pltpu.VMEM(norm_gain.shape, jnp.bfloat16),
            pltpu.VMEM(tokens.shape, jnp.int32),
            pltpu.VMEM((models, steps * own, features), jnp.float32),
            pltpu.VMEM((CHUNKS, PLANE, CORES, DEPTH, steps * own, width), jnp.bfloat16),
            pltpu.VMEM((CHUNKS, width, columns), jnp.bfloat16),
            pltpu.VMEM((models, steps * rows, columns), jnp.float32),
            pltpu.VMEM((steps, rows, columns), jnp.bfloat16),
            pltpu.VMEM((steps, rows, rows), jnp.float32),
            pltpu.VMEM((3, steps, rows, rows), jnp.float32),
            pltpu.VMEM((DEPTH, 3 * steps, rows), jnp.float32),
            pltpu.VMEM((PLANE * CORES, 3 * steps, rows), jnp.float32),
            one_sem,
            one_sem,
            one_sem,
            chunk_sems,
            one_sem,
        ]
        + [each_sems] * 2
        + [chunk_sems] * 8
        + [each_sems] * 2
        + [line_sems] * 2
        + [plane_sems] * 2,
        compiler_params=pltpu.CompilerParams(
            collective_id=0, has_side_effects=True, vmem_limit_bytes=40 << 20
        ),
        name="experts",
    )(*[pltpu.with_memory_space_constraint(value, pltpu.HBM) for value in (hidden, norm_gain, head_weight, base_logits, tokens)])
    log_probs, chosen, ranking = pl.pallas_call(
        finish_kernel,
        out_shape=(
            jax.ShapeDtypeStruct((steps, rows, columns), jnp.float32),
            jax.ShapeDtypeStruct((steps, rows), jnp.float32),
            jax.ShapeDtypeStruct((1, rows), jnp.float32),
        ),
        in_specs=[local] * 3,
        out_specs=(far, local, local),
        scratch_shapes=[
            pltpu.VMEM((steps, rows, columns), jnp.float32),
            pltpu.SemaphoreType.DMA((steps,)),
        ],
        compiler_params=pltpu.CompilerParams(vmem_limit_bytes=16 << 20),
        name="finish",
    )(combined, merged, cache_length.reshape(1, rows))
    return (log_probs, chosen, ranking.reshape(rows))


def fits_box(mesh):
    return mesh.shape["replica"] == 1 and mesh.shape["sub"] == 1 and mesh.shape["mp"] == PLANE * DEPTH * CORES


def solution(mesh):
    return jax.shard_map(
        on_box if fits_box(mesh) else on_device,
        mesh=mesh,
        in_specs=(
            P(None, ("replica", "mp"), "sub", None),
            P("sub", None),
            P("sub", None, "mp"),
            P(None, ("replica", "sub"), "mp"),
            P(None, ("replica", "sub")),
            P(("replica", "sub")),
        ),
        out_specs=(
            P(None, ("replica", "sub"), "mp"),
            P(None, ("replica", "sub")),
            P(("replica", "sub")),
        ),
        check_vma=False,
    )
```

```python
import functools

import jax
import jax.numpy as jnp
from jax import lax
from jax.experimental import pallas as pl
from jax.experimental.pallas import tpu as pltpu
from jax.sharding import PartitionSpec as P

ALPHA = 2.0
EPSILON = 1e-05


def score_block(normed, base_block, token_block, weights, slice_start):
    logits = jnp.einsum(
        "srmd,mdv->smrv",
        lax.all_gather(normed, "mp", axis=1, tiled=True),
        weights,
        preferred_element_type=jnp.float32,
    ).astype(jnp.bfloat16)
    step_count, model_count, row_count, vocab_width = logits.shape
    groups = lax.axis_size("sub")
    shares = logits.reshape(step_count, model_count, groups, row_count // groups, vocab_width)
    paired = lax.all_to_all(shares, "sub", split_axis=2, concat_axis=1, tiled=True)
    paired = paired.reshape(step_count, 2, row_count // groups, vocab_width)
    combined = base_block.astype(jnp.float32) + ALPHA * (
        paired[:, 0].astype(jnp.float32) - paired[:, 1].astype(jnp.float32)
    )
    columns = lax.broadcasted_iota(jnp.int32, (1, 1, vocab_width), 2) + slice_start
    picked_part = jnp.sum(jnp.where(columns == token_block[:, :, None], combined, 0.0), axis=2)
    maximum = lax.pmax(jnp.max(combined, axis=2), "mp")
    partial_value = jnp.sum(jnp.exp(combined - maximum[:, :, None]), axis=2)
    summed, picked = lax.psum((partial_value, picked_part), "mp")
    log_summed = jnp.log(summed)
    log_block = combined - maximum[:, :, None] - log_summed[:, :, None]
    chosen_block = picked - maximum - log_summed
    return (log_block, chosen_block)


def on_device(hidden, norm_gain, head_weight, base_logits, tokens, cache_length):
    step_count = hidden.shape[0]
    slice_start = lax.axis_index("mp") * head_weight.shape[2]
    values = hidden.astype(jnp.float32)
    mean_square = jnp.mean(values * values, axis=-1, keepdims=True)
    normed = (
        values * lax.rsqrt(mean_square + EPSILON) * norm_gain.astype(jnp.float32)[None, None]
    ).astype(jnp.bfloat16)
    log_parts = []
    chosen_parts = []
    for moment in range(step_count):
        log_block, chosen_block = score_block(
            normed[moment : moment + 1],
            base_logits[moment : moment + 1],
            tokens[moment : moment + 1],
            head_weight,
            slice_start,
        )
        log_parts.append(log_block)
        chosen_parts.append(chosen_block)
    log_probs = jnp.concatenate(log_parts, axis=0)
    chosen = jnp.concatenate(chosen_parts, axis=0)
    penalty = ((5.0 + cache_length.astype(jnp.float32) + step_count) / 6.0) ** 0.6
    ranking = jnp.sum(chosen, axis=0) / penalty
    return (log_probs, chosen, ranking)

CHUNKS = 8
AHEAD = 2
PLANE = 4
DEPTH = 4
CORES = 2


def remote(source, target, send_sem, recv_sem, device):
    return pltpu.make_async_remote_copy(
        src_ref=source,
        dst_ref=target,
        send_sem=send_sem,
        recv_sem=recv_sem,
        device_id={"mp": device},
        device_id_type=pl.DeviceIdType.MESH,
    )


def diagonal_of(rows):
    return lax.broadcasted_iota(jnp.int32, (rows, rows), 0) == lax.broadcasted_iota(jnp.int32, (rows, rows), 1)


def to_column(line, diagonal):
    square = jnp.broadcast_to(line, diagonal.shape)
    return jnp.sum(jnp.where(diagonal, square, 0.0), axis=1, keepdims=True)


def finish_kernel(combined, merged, cache_length, out_hbm, chosen_out, ranking_out, out, out_sem):
    steps, rows = chosen_out.shape
    diagonal = diagonal_of(rows)
    log_total = jnp.log(merged[steps : 2 * steps, :])
    copies = []
    for step in range(steps):
        peak_column = to_column(merged[step : step + 1, :], diagonal)
        log_column = to_column(log_total[step : step + 1, :], diagonal)
        out[step] = (combined[step] - peak_column) - log_column
        copies.append(pltpu.make_async_copy(out.at[step], out_hbm.at[step], out_sem.at[step]))
        copies[-1].start()
    chosen = (merged[2 * steps : 3 * steps, :] - merged[0:steps, :]) - log_total
    chosen_out[...] = chosen
    penalty = jnp.exp(0.6 * jnp.log((5.0 + cache_length[...].astype(jnp.float32) + steps) / 6.0))
    ranking_out[...] = jnp.sum(chosen, axis=0, keepdims=True) / penalty
    for copy in copies:
        copy.wait()


def expert_kernel(
    hidden_hbm,
    gain_hbm,
    weight_hbm,
    base_hbm,
    tokens_hbm,
    out,
    merged_out,
    hidden,
    gain,
    tokens,
    values,
    gathered,
    weight,
    acc,
    base,
    token_columns,
    stats,
    line_stats,
    plane_stats,
    hidden_sem,
    gain_sem,
    tokens_sem,
    weight_sem,
    base_sem,
    z_send,
    z_recv,
    x_send,
    x_recv,
    y_send,
    y_recv,
    dx_send,
    dx_recv,
    dy_send,
    dy_recv,
    s_send,
    s_recv,
    line_send,
    line_recv,
    plane_send,
    plane_recv,
):
    me = lax.axis_index("mp")
    z = me // 8
    q = (me // 2) % 4
    c = me % 2
    qx = q + 1 - 2 * (q % 2)
    qy = (q + 2) % 4
    qd = qx + 2 - 4 * (qx // 2)

    def device(zz, qq, cc):
        return zz * 8 + qq * 2 + cc

    x_device = device(z, qx, c)
    y_device = device(z, qy, c)
    sibling = device(z, q, 1 - c)
    blocks = CHUNKS // 2
    width = gathered.shape[5]
    hidden_copy = pltpu.make_async_copy(hidden_hbm, hidden, hidden_sem)
    gain_copy = pltpu.make_async_copy(gain_hbm, gain, gain_sem)
    tokens_copy = pltpu.make_async_copy(tokens_hbm, tokens, tokens_sem)
    hidden_copy.start()
    gain_copy.start()

    def weight_copy(chunk):
        return pltpu.make_async_copy(
            weight_hbm.at[chunk // blocks, pl.ds((chunk % blocks) * width, width), :],
            weight.at[chunk],
            weight_sem.at[chunk],
        )

    base_copy = pltpu.make_async_copy(base_hbm, base, base_sem)

    def z_copy(chunk, shift):
        peer = (z + shift) % DEPTH
        return remote(
            gathered.at[chunk, q, c, z], gathered.at[chunk, q, c, z], z_send.at[chunk, peer], z_recv.at[chunk, z], device(peer, q, c)
        )

    def z_arrival(chunk, shift):
        peer = (z + shift) % DEPTH
        return remote(
            gathered.at[chunk, q, c, peer], gathered.at[chunk, q, c, peer], z_send.at[chunk, peer], z_recv.at[chunk, peer], device(peer, q, c)
        )

    def block_copy(chunk, block, send_sem, recv_sem, target):
        place = gathered.at[chunk, block, c]
        return remote(place, place, send_sem.at[chunk], recv_sem.at[chunk], target)

    def half_copy(chunk, block, start, send_sem, recv_sem, target):
        place = gathered.at[chunk, block, c, pl.ds(start, DEPTH // 2)]
        return remote(place, place, send_sem.at[chunk], recv_sem.at[chunk], target)

    def sibling_copy(chunk, block, core):
        place = gathered.at[chunk, block, core]
        return remote(place, place, s_send.at[chunk, block], s_recv.at[chunk, block], sibling)

    barrier = pltpu.get_barrier_semaphore()
    for shift in range(1, DEPTH):
        pl.semaphore_signal(barrier, inc=1, device_id={"mp": device((z + shift) % DEPTH, q, c)}, device_id_type=pl.DeviceIdType.MESH)
    for shift in range(1, PLANE * CORES):
        other = (me % 8 + shift) % 8
        pl.semaphore_signal(barrier, inc=1, device_id={"mp": z * 8 + other}, device_id_type=pl.DeviceIdType.MESH)

    @pl.loop(0, CHUNKS)
    def _(chunk):
        weight_copy(chunk).start()

    base_copy.start()
    tokens_copy.start()
    hidden_copy.wait()
    gain_copy.wait()
    steps, own, models, features = hidden.shape
    for row in range(steps * own):
        pair = hidden[row // own, row % own].astype(jnp.float32)
        for model in range(models):
            values[model, row : row + 1, :] = pair[model : model + 1, :]
    for model in range(models):
        value = values[model]
        mean_square = jnp.mean(value * value, axis=-1, keepdims=True)
        scaled = value * lax.rsqrt(mean_square + EPSILON) * gain[model : model + 1, :].astype(jnp.float32)
        for part in range(blocks):
            gathered[model * blocks + part, q, c, z] = scaled[:, part * width : (part + 1) * width].astype(jnp.bfloat16)
    pl.semaphore_wait(barrier, DEPTH - 1 + PLANE * CORES - 1)
    for chunk in range(AHEAD):
        for shift in range(1, DEPTH):
            z_copy(chunk, shift).start()
    tokens_copy.wait()
    rows, columns = out.shape[1:]
    diagonal = diagonal_of(rows)

    def to_line(square):
        return jnp.sum(jnp.where(diagonal, square, 0.0), axis=0, keepdims=True)

    for step in range(steps):
        token_columns[step] = jnp.broadcast_to(to_column(tokens[step : step + 1, :].astype(jnp.float32), diagonal), (rows, rows))

    @pl.loop(0, CHUNKS + 3)
    def _(tick):
        @pl.when(tick < CHUNKS)
        def _():
            chunk = tick
            for shift in range(1, DEPTH):
                z_arrival(chunk, shift).wait_recv()
            block_copy(chunk, q, x_send, x_recv, x_device).start()
            block_copy(chunk, q, y_send, y_recv, y_device).start()
            sibling_copy(chunk, q, c).start()

        @pl.when(tick < CHUNKS - AHEAD)
        def _():
            for shift in range(1, DEPTH):
                z_copy(tick + AHEAD, shift).start()

        @pl.when(tick >= 3)
        def _():
            chunk = tick - 3
            for block in range(PLANE):
                sibling_copy(chunk, block, 1 - c).wait_recv()
            weight_copy(chunk).wait()
            model = chunk // blocks
            part = chunk % blocks
            count = gathered.shape[1] * gathered.shape[2] * gathered.shape[3] * gathered.shape[4]
            left = gathered[chunk].reshape(count, width)

            @pl.loop(0, columns // 256)
            def _(tile):
                at = pl.ds(pl.multiple_of(tile * 256, 256), 256)
                product = jnp.dot(left, weight[chunk, :, at], preferred_element_type=jnp.float32)

                @pl.when(part == 0)
                def _():
                    acc[model, :, at] = product

                @pl.when(part > 0)
                def _():
                    acc[model, :, at] += product

        @pl.when(jnp.logical_and(tick >= 1, tick < CHUNKS + 1))
        def _():
            chunk = tick - 1
            block_copy(chunk, qx, x_send, x_recv, x_device).wait_recv()
            half_copy(chunk, qx, 0, dy_send, dy_recv, y_device).start()
            block_copy(chunk, qy, y_send, y_recv, y_device).wait_recv()
            half_copy(chunk, qy, DEPTH // 2, dx_send, dx_recv, x_device).start()
            sibling_copy(chunk, qx, c).start()
            sibling_copy(chunk, qy, c).start()

        @pl.when(jnp.logical_and(tick >= 2, tick < CHUNKS + 2))
        def _():
            chunk = tick - 2
            half_copy(chunk, qd, 0, dy_send, dy_recv, y_device).wait_recv()
            half_copy(chunk, qd, DEPTH // 2, dx_send, dx_recv, x_device).wait_recv()
            sibling_copy(chunk, qd, c).start()

    base_copy.wait()
    slice_start = me * columns
    column = (lax.broadcasted_iota(jnp.int32, (16, columns), 1) + slice_start).astype(jnp.float32)
    low = lax.broadcasted_iota(jnp.int32, (8, columns), 0) < 4

    @pl.loop(0, rows // 16)
    def _(group):
        zz = group // 2
        pair = group % 2
        first = pl.multiple_of(group * 16, 16)
        parts = [[] for _ in range(steps)]
        for block in range(2):
            for tile in range(steps // 2):
                values = []
                for core in range(CORES):
                    place = pl.multiple_of((((pair * 2 + block) * CORES + core) * DEPTH + zz) * 16 + tile * 8, 8)
                    expert = acc[0, pl.ds(place, 8), :].astype(jnp.bfloat16).astype(jnp.float32)
                    anti = acc[1, pl.ds(place, 8), :].astype(jnp.bfloat16).astype(jnp.float32)
                    values.append(ALPHA * (expert - anti))
                parts[2 * tile].append(jnp.where(low, values[0], pltpu.roll(values[1], 4, 0)))
                parts[2 * tile + 1].append(jnp.where(low, pltpu.roll(values[0], 4, 0), values[1]))
        for step in range(steps):
            combined = base[step, pl.ds(first, 16), :].astype(jnp.float32) + jnp.concatenate(parts[step], axis=0)
            out[step, pl.ds(first, 16), :] = combined
            peak = jnp.max(combined, axis=1, keepdims=True)
            total = jnp.sum(jnp.exp(combined - peak), axis=1, keepdims=True)
            token = token_columns[step, pl.ds(first, 16), :][:, 0:1]
            picked = jnp.sum(jnp.where(column == token, combined, 0.0), axis=1, keepdims=True)
            stats[0, step, pl.ds(first, 16), :] = jnp.broadcast_to(peak, (16, rows))
            stats[1, step, pl.ds(first, 16), :] = jnp.broadcast_to(total, (16, rows))
            stats[2, step, pl.ds(first, 16), :] = jnp.broadcast_to(picked, (16, rows))

    for kind in range(3):
        for step in range(steps):
            line_stats[z, pl.ds(kind * steps + step, 1), :] = to_line(stats[kind, step])

    def line_copy(shift):
        peer = (z + shift) % DEPTH
        return remote(line_stats.at[z], line_stats.at[z], line_send.at[peer], line_recv.at[z], device(peer, q, c))

    def line_arrival(shift):
        peer = (z + shift) % DEPTH
        return remote(line_stats.at[peer], line_stats.at[peer], line_send.at[peer], line_recv.at[peer], device(peer, q, c))

    spot = me % 8

    def plane_copy(shift):
        peer = (spot + shift) % 8
        return remote(plane_stats.at[spot], plane_stats.at[spot], plane_send.at[peer], plane_recv.at[spot], z * 8 + peer)

    def plane_arrival(shift):
        peer = (spot + shift) % 8
        return remote(plane_stats.at[peer], plane_stats.at[peer], plane_send.at[peer], plane_recv.at[peer], z * 8 + peer)

    def merge(ref, count):
        peaks = [ref[index, 0:steps, :] for index in range(count)]
        peak = functools.reduce(jnp.maximum, peaks)
        total = sum(ref[index, steps : 2 * steps, :] * jnp.exp(peaks[index] - peak) for index in range(count))
        picked = sum(ref[index, 2 * steps : 3 * steps, :] for index in range(count))
        return peak, total, picked

    for shift in range(1, DEPTH):
        line_copy(shift).start()
    for shift in range(1, DEPTH):
        line_arrival(shift).wait_recv()
    for index, value in enumerate(merge(line_stats, DEPTH)):
        plane_stats[spot, pl.ds(index * steps, steps), :] = value
    for shift in range(1, 8):
        plane_copy(shift).start()
    for shift in range(1, 8):
        plane_arrival(shift).wait_recv()
    for index, value in enumerate(merge(plane_stats, 8)):
        merged_out[index * steps : (index + 1) * steps, :] = value

    for shift in range(1, DEPTH):
        line_copy(shift).wait_send()
    for shift in range(1, 8):
        plane_copy(shift).wait_send()

    @pl.loop(0, CHUNKS)
    def _(chunk):
        for shift in range(1, DEPTH):
            z_copy(chunk, shift).wait_send()
        block_copy(chunk, q, x_send, x_recv, x_device).wait_send()
        block_copy(chunk, q, y_send, y_recv, y_device).wait_send()
        half_copy(chunk, qx, 0, dy_send, dy_recv, y_device).wait_send()
        half_copy(chunk, qy, DEPTH // 2, dx_send, dx_recv, x_device).wait_send()
        for block in range(PLANE):
            sibling_copy(chunk, block, c).wait_send()


def on_box(hidden, norm_gain, head_weight, base_logits, tokens, cache_length):
    steps, own, models, features = hidden.shape
    rows, columns = base_logits.shape[1:]
    width = features * models // CHUNKS
    far = pl.BlockSpec(memory_space=pltpu.HBM)
    local = pl.BlockSpec(memory_space=pltpu.VMEM)
    chunk_sems = pltpu.SemaphoreType.DMA((CHUNKS,))
    line_sems = pltpu.SemaphoreType.DMA((DEPTH,))
    plane_sems = pltpu.SemaphoreType.DMA((PLANE * CORES,))
    each_sems = pltpu.SemaphoreType.DMA((CHUNKS, DEPTH))
    one_sem = pltpu.SemaphoreType.DMA
    combined, merged = pl.pallas_call(
        expert_kernel,
        out_shape=(
            jax.ShapeDtypeStruct((steps, rows, columns), jnp.float32),
            jax.ShapeDtypeStruct((3 * steps, rows), jnp.float32),
        ),
        in_specs=[far] * 5,
        out_specs=(local, local),
        scratch_shapes=[
            pltpu.VMEM(hidden.shape, jnp.bfloat16),
            pltpu.VMEM(norm_gain.shape, jnp.bfloat16),
            pltpu.VMEM(tokens.shape, jnp.int32),
            pltpu.VMEM((models, steps * own, features), jnp.float32),
            pltpu.VMEM((CHUNKS, PLANE, CORES, DEPTH, steps * own, width), jnp.bfloat16),
            pltpu.VMEM((CHUNKS, width, columns), jnp.bfloat16),
            pltpu.VMEM((models, steps * rows, columns), jnp.float32),
            pltpu.VMEM((steps, rows, columns), jnp.bfloat16),
            pltpu.VMEM((steps, rows, rows), jnp.float32),
            pltpu.VMEM((3, steps, rows, rows), jnp.float32),
            pltpu.VMEM((DEPTH, 3 * steps, rows), jnp.float32),
            pltpu.VMEM((PLANE * CORES, 3 * steps, rows), jnp.float32),
            one_sem,
            one_sem,
            one_sem,
            chunk_sems,
            one_sem,
        ]
        + [each_sems] * 2
        + [chunk_sems] * 8
        + [each_sems] * 2
        + [line_sems] * 2
        + [plane_sems] * 2,
        compiler_params=pltpu.CompilerParams(
            collective_id=0, has_side_effects=True, vmem_limit_bytes=40 << 20
        ),
        name="experts",
    )(*[pltpu.with_memory_space_constraint(value, pltpu.HBM) for value in (hidden, norm_gain, head_weight, base_logits, tokens)])
    log_probs, chosen, ranking = pl.pallas_call(
        finish_kernel,
        out_shape=(
            jax.ShapeDtypeStruct((steps, rows, columns), jnp.float32),
            jax.ShapeDtypeStruct((steps, rows), jnp.float32),
            jax.ShapeDtypeStruct((1, rows), jnp.float32),
        ),
        in_specs=[local] * 3,
        out_specs=(far, local, local),
        scratch_shapes=[
            pltpu.VMEM((steps, rows, columns), jnp.float32),
            pltpu.SemaphoreType.DMA((steps,)),
        ],
        compiler_params=pltpu.CompilerParams(vmem_limit_bytes=16 << 20),
        name="finish",
    )(combined, merged, cache_length.reshape(1, rows))
    return (log_probs, chosen, ranking.reshape(rows))


def fits_box(mesh):
    return mesh.shape["replica"] == 1 and mesh.shape["sub"] == 1 and mesh.shape["mp"] == PLANE * DEPTH * CORES


def solution(mesh):
    return jax.shard_map(
        on_box if fits_box(mesh) else on_device,
        mesh=mesh,
        in_specs=(
            P(None, ("replica", "mp"), "sub", None),
            P("sub", None),
            P("sub", None, "mp"),
            P(None, ("replica", "sub"), "mp"),
            P(None, ("replica", "sub")),
            P(("replica", "sub")),
        ),
        out_specs=(
            P(None, ("replica", "sub"), "mp"),
            P(None, ("replica", "sub")),
            P(("replica", "sub")),
        ),
        check_vma=False,
    )
```
